256 devices in a mesh: patch: 16 (over x_hi, z), depth: 16 (over y, x_lo, core).
Axes of the slice: x: 4 (x_hi: 2, x_lo: 2; x = x_hi * 2 + x_lo), y: 4, z: 8, core: 2. Of those that a mesh axis runs over, the one named last changes fastest.
Arguments:
- slabs: bfloat16 [16, 32, 16, 32, 384], P('patch', 'depth'), may hold values from -12 to 12, as said below
- kernel: bfloat16 [3, 3, 3, 384, 384], P(None, None, None, None, 'patch'), may hold values from -0.0625 to 0.0625
- gain: float32 [384], replicated, may hold values from 0.25 to 1.75
- shift: float32 [384], replicated, may hold values from -3 to 3
Outputs:
- activated: bfloat16 [16, 32, 16, 32, 384], P('patch', 'depth')
The draws below stay inside these ranges and needn't reach their ends.
Inputs may be any that keep to these rules, and one draw needn't show every extreme that they name: `slabs`: feature values of order one.
All inputs are finite; a program needn't handle non-finite values.
Results may differ from the reference program's by a relative error of at most 0.001.
Values may be sent and summed in bfloat16 or wider, within the bound.
No kernel may reach another device: no remote copies, remote signals or barrier semaphores. Data moves between devices by JAX's collectives and lax.ppermute only.
A program may use at most 384 MiB of HBM per device.

```python
import jax
import jax.numpy as jnp
from jax import lax

C = 384
H = 16
W = 32
NZ = 32
PATCHES = 16


def draw_slabs(key, part):
    first, second = jax.random.split(key)
    planes = jnp.arange(NZ, dtype=jnp.float32)
    scale = 1.0 + 2.0 * planes / max(NZ - 1, 1)
    noise = jax.random.normal(first, (PATCHES, NZ, H, W, C), jnp.float32)
    offset = 0.5 * jax.random.normal(second, (PATCHES, 1, 1, 1, C), jnp.float32)
    values = scale[None, :, None, None, None] * (noise + offset)
    return jnp.clip(values, -12.0, 12.0).astype(jnp.bfloat16)


def block_levels(stream_key, dims, shards, low, top_value):
    def one(position, shards_of):
        steps = jax.random.uniform(jax.random.fold_in(jax.random.fold_in(stream_key, 6), position), (shards_of,), jnp.float32, low / len(shards), top_value / len(shards))
        return jnp.repeat(jnp.exp(steps), dims[position] // shards_of).reshape((-1,) + (1,) * (len(dims) - position - 1))

    factor_of = one(*shards[0])
    for cut in shards[1:]:
        factor_of = factor_of * one(*cut)
    return factor_of


def scatter_about(key, shape, width, bound, cuts=(), held_as=jnp.bfloat16):
    drawn = width * jax.random.normal(key, shape, jnp.float32)
    if cuts:
        drawn = drawn * block_levels(key, shape, cuts, -0.22, 0.18)
    return jnp.clip(drawn, -bound, bound).astype(held_as)


def setup_inputs(seed: int = 0) -> dict:
    key_list = jax.random.split(jax.random.key(seed), 5)
    return {
        "slabs": draw_slabs(jax.random.fold_in(key_list[4], 71), 0),
        "kernel": scatter_about(key_list[1], (3, 3, 3, C, C), (27 * C) ** -0.5, 0.0625, ((4, 16),)),
        "gain": jnp.clip(1.0 + 0.15 * jax.random.normal(key_list[2], (C,), jnp.float32), 0.25, 1.75),
        "shift": scatter_about(key_list[3], (C,), 0.5, 3.0, (), jnp.float32),
    }


def reference(slabs, kernel, gain, shift):
    weights = kernel.astype(jnp.float32)

    def one_patch(volume):
        conv_out = lax.conv_general_dilated(volume[None].astype(jnp.float32), weights, (1, 1, 1), 'SAME', dimension_numbers=('NDHWC', 'DHWIO', 'NDHWC'), precision=lax.Precision.HIGHEST)[0]
        mean = lax.optimization_barrier(jnp.mean(conv_out, axis=(0, 1, 2)))
        meansq = lax.optimization_barrier(jnp.mean(conv_out * conv_out, axis=(0, 1, 2)))
        variance = meansq - mean * mean
        normed = gain * (conv_out - mean) / jnp.sqrt(variance + 1e-05) + shift
        return jnp.where(normed >= 0, normed, 0.01 * normed).astype(jnp.bfloat16)
    return lax.map(one_patch, slabs)
```

```python
import functools

import jax
import jax.numpy as jnp
from jax import lax
from jax.experimental import pallas as pl
from jax.experimental.pallas import tpu as pltpu
from jax.sharding import Mesh, PartitionSpec as P

AXES = ("xh", "z", "y", "xl", "c")
SIZES = (2, 8, 4, 2, 2)
CHIPS = ("y", "xl")
DEPTH = ("y", "xl", "c")
SWAP = [(0, 1), (1, 0)]
EPS = 1e-05


def shift_rows(plane, by, width):
    rows = plane.shape[0]
    moved = pltpu.roll(plane, by % rows, 0)
    w = lax.broadcasted_iota(jnp.int32, plane.shape, 0) % width
    edge = 0 if by == 1 else width - 1
    return jnp.where(w == edge, 0.0, moved)


def widen_kernel(x_ref, o_ref, *, width):
    x = x_ref[0]
    rows, chans = x.shape
    zero = jnp.zeros((width, 3 * chans), o_ref.dtype)
    o_ref[0, 0:width, :] = zero
    o_ref[0, width + rows : 2 * width + rows, :] = zero
    wide = x.astype(jnp.float32)
    o_ref[0, width : width + rows, 0:chans] = shift_rows(wide, 1, width).astype(o_ref.dtype)
    o_ref[0, width : width + rows, chans : 2 * chans] = x
    o_ref[0, width : width + rows, 2 * chans : 3 * chans] = shift_rows(wide, -1, width).astype(o_ref.dtype)


def widen(planes, width):
    count, rows, chans = planes.shape
    return pl.pallas_call(
        functools.partial(widen_kernel, width=width),
        grid=(count,),
        in_specs=[pl.BlockSpec((1, rows, chans), lambda i: (i, 0, 0))],
        out_specs=pl.BlockSpec((1, rows + 2 * width, 3 * chans), lambda i: (i, 0, 0)),
        out_shape=jax.ShapeDtypeStruct((count, rows + 2 * width, 3 * chans), planes.dtype),
        compiler_params=pltpu.CompilerParams(vmem_limit_bytes=32 << 20),
        cost_estimate=pl.CostEstimate(flops=0, bytes_accessed=12_000_000, transcendentals=0),
    )(planes)


def conv_kernel(core_ref, x_ref, w_ref, send_ref, keep_ref, stats_ref, acc_ref, *, rows, width):
    del core_ref
    j, a = pl.program_id(0), pl.program_id(1)
    lhs = jnp.concatenate([x_ref[0, b * width : b * width + rows, :] for b in range(3)], axis=1)
    rhs = jnp.concatenate([w_ref[0, t] for t in range(9)], axis=1)
    part = lax.dot_general(lhs, rhs, (((1,), (1,)), ((), ())), preferred_element_type=jnp.float32)

    @pl.when(a == 0)
    def _():
        acc_ref[...] = part

    @pl.when(a == 1)
    def _():
        acc_ref[...] += part

    @pl.when((j == 0) & (a == 0))
    def _():
        stats_ref[...] = jnp.zeros_like(stats_ref)

    @pl.when(a == 2)
    def _():
        total = acc_ref[...] + part
        stats_ref[0:1, :] += jnp.sum(total, axis=0, keepdims=True)
        stats_ref[1:2, :] += jnp.sum(total * total, axis=0, keepdims=True)

        @pl.when(j < 2)
        def _():
            send_ref[0] = total

        @pl.when(j >= 2)
        def _():
            keep_ref[0] = total


def conv(core, wide, weights, rows, width):
    outs = weights.shape[2]
    part = jax.ShapeDtypeStruct((2, rows, outs), jnp.float32)
    spec = pltpu.PrefetchScalarGridSpec(
        num_scalar_prefetch=1,
        grid=(4, 3),
        in_specs=[
            pl.BlockSpec((1, wide.shape[1], wide.shape[2]), lambda j, a, core: ((j + 2 * (1 - core[0])) % 4 + a, 0, 0)),
            pl.BlockSpec((1, 9, outs, weights.shape[3]), lambda j, a, core: (a, 0, 0, 0)),
        ],
        out_specs=[
            pl.BlockSpec((1, rows, outs), lambda j, a, core: (jnp.minimum(j, 1), 0, 0)),
            pl.BlockSpec((1, rows, outs), lambda j, a, core: (jnp.maximum(j - 2, 0), 0, 0)),
            pl.BlockSpec((8, outs), lambda j, a, core: (0, 0)),
        ],
        scratch_shapes=[pltpu.VMEM((rows, outs), jnp.float32)],
    )
    return pl.pallas_call(
        functools.partial(conv_kernel, rows=rows, width=width),
        grid_spec=spec,
        out_shape=[part, part, jax.ShapeDtypeStruct((8, outs), jnp.float32)],
        compiler_params=pltpu.CompilerParams(vmem_limit_bytes=40 << 20),
        cost_estimate=pl.CostEstimate(flops=8 * 10**9, bytes_accessed=16_000_000, transcendentals=0),
    )(core, wide, weights)


def norm_kernel(core_ref, keep_ref, recv_ref, sums_ref, gain_ref, shift_ref, o_ref, *, cells):
    first = core_ref[0] == 0
    outs = keep_ref.shape[2]
    keep, recv = keep_ref[0], recv_ref[0]
    for half in range(2):
        mean = sums_ref[half, 0:1, :] / cells
        variance = sums_ref[half, 1:2, :] / cells - mean * mean
        scale = gain_ref[half] / jnp.sqrt(variance + EPS)
        conv_out = jnp.where(first, keep, recv) if half == 0 else jnp.where(first, recv, keep)
        normed = (conv_out - mean) * scale + shift_ref[half]
        active = jnp.where(normed >= 0, normed, 0.01 * normed).astype(o_ref.dtype)
        o_ref[0, :, half * outs : (half + 1) * outs] = active


def normalize(core, keep, recv, sums, gain, shift, cells):
    planes, rows, outs = keep.shape
    tile = 256
    spec = pltpu.PrefetchScalarGridSpec(
        num_scalar_prefetch=1,
        grid=(planes, rows // tile),
        in_specs=[
            pl.BlockSpec((1, tile, outs), lambda i, j, core: (i, j, 0)),
            pl.BlockSpec((1, tile, outs), lambda i, j, core: (i, j, 0)),
            pl.BlockSpec((2, 2, outs), lambda i, j, core: (0, 0, 0)),
            pl.BlockSpec((2, 1, outs), lambda i, j, core: (0, 0, 0)),
            pl.BlockSpec((2, 1, outs), lambda i, j, core: (0, 0, 0)),
        ],
        out_specs=pl.BlockSpec((1, tile, 2 * outs), lambda i, j, core: (i, j, 0)),
    )
    return pl.pallas_call(
        functools.partial(norm_kernel, cells=cells),
        grid_spec=spec,
        out_shape=jax.ShapeDtypeStruct((planes, rows, 2 * outs), jnp.bfloat16),
        compiler_params=pltpu.CompilerParams(vmem_limit_bytes=32 << 20),
        cost_estimate=pl.CostEstimate(flops=4_000_000, bytes_accessed=3_000_000, transcendentals=0),
    )(core, keep, recv, sums, gain, shift)


def chip_planes(slab, core):
    other = lax.ppermute(slab, "c", SWAP)
    inner = jnp.where(core == 0, jnp.concatenate([slab, other]), jnp.concatenate([other, slab]))
    chips = SIZES[2] * SIZES[3]
    before = lax.ppermute(inner[3:], CHIPS, [(i, i + 1) for i in range(chips - 1)])
    after = lax.ppermute(inner[:1], CHIPS, [(i + 1, i) for i in range(chips - 1)])
    return jnp.concatenate([before, inner, after])


def x_exchange(shard, core):
    pairs = []
    for xl in range(2):
        low, high = (0 + xl) * 2 + 1, (2 + 1 - xl) * 2
        pairs += [(low, high), (high, low)]
    other = lax.ppermute(shard, ("xh", "xl", "c"), pairs)
    return jnp.where(core == lax.axis_index("xh"), shard, other)


def local(slabs, kernel, gain, shift):
    core = lax.axis_index("c")
    core_arg = core.reshape(1).astype(jnp.int32)
    _, planes, height, width, chans = slabs.shape
    rows = height * width
    outs = chans // 2

    shard = jnp.transpose(kernel, (0, 1, 2, 4, 3)).reshape(27, kernel.shape[4], chans)
    half = lax.all_gather(x_exchange(shard, core), "z", axis=1, tiled=True)
    weights = half.reshape(3, 9, outs, chans)

    wide = widen(chip_planes(slabs[0].reshape(planes, rows, chans), core), width)
    send, keep, stats = conv(core_arg, wide, weights, rows, width)

    recv = lax.ppermute(send, "c", SWAP)
    mine = stats[:2].reshape(1, 2 * outs)
    group = SIZES[2] * SIZES[3] * SIZES[4]
    everyone = lax.all_to_all(jnp.broadcast_to(mine, (group, 2 * outs)), DEPTH, 0, 0)
    sums = jnp.sum(everyone.reshape(group // 2, 2, 2, outs), axis=0)
    cells = planes * rows * group
    out = normalize(
        core_arg, keep, recv, sums, gain.reshape(2, 1, outs), shift.reshape(2, 1, outs), cells
    )
    return out.reshape(slabs.shape)


def solution(mesh):
    fine = Mesh(mesh.devices.reshape(SIZES), AXES)
    x_spec = P(("xh", "z"), DEPTH, None, None, None)
    in_specs = (x_spec, P(None, None, None, None, ("xh", "z")), P(), P())
    return jax.shard_map(local, mesh=fine, in_specs=in_specs, out_specs=x_spec, check_vma=False)
```

```python
import functools
import math

import jax
import jax.numpy as jnp
from jax import lax
from jax.experimental import pallas as pl
from jax.experimental.pallas import tpu as pltpu
from jax.sharding import Mesh, PartitionSpec as P

AXES = ("xh", "z", "y", "xl", "c")
SIZES = (2, 8, 4, 2, 2)
CHIPS = ("y", "xl")
DEPTH = ("y", "xl", "c")
SWAP = [(0, 1), (1, 0)]
EPS = 1e-05
PADDED = 256
QUARTER_START = (0, 7, 14, 20)


def quarter_of(tap):
    return min(tap // 7, 3)


def shift_rows(plane, by, width):
    rows = plane.shape[0]
    moved = pltpu.roll(plane, by % rows, 0)
    w = lax.broadcasted_iota(jnp.int32, plane.shape, 0) % width
    edge = 0 if by == 1 else width - 1
    return jnp.where(w == edge, 0.0, moved)


def widen_kernel(x_ref, o_ref, *, width):
    x = x_ref[0]
    rows, chans = x.shape
    zero = jnp.zeros((width, 3 * chans), o_ref.dtype)
    o_ref[0, 0:width, :] = zero
    o_ref[0, width + rows : 2 * width + rows, :] = zero
    wide = x.astype(jnp.float32)
    o_ref[0, width : width + rows, 0:chans] = shift_rows(wide, 1, width).astype(o_ref.dtype)
    o_ref[0, width : width + rows, chans : 2 * chans] = x
    o_ref[0, width : width + rows, 2 * chans : 3 * chans] = shift_rows(wide, -1, width).astype(o_ref.dtype)


def widen(planes, width):
    count, rows, chans = planes.shape
    return pl.pallas_call(
        functools.partial(widen_kernel, width=width),
        grid=(count,),
        in_specs=[pl.BlockSpec((1, rows, chans), lambda i: (i, 0, 0))],
        out_specs=pl.BlockSpec((1, rows + 2 * width, 3 * chans), lambda i: (i, 0, 0)),
        out_shape=jax.ShapeDtypeStruct((count, rows + 2 * width, 3 * chans), planes.dtype),
        compiler_params=pltpu.CompilerParams(vmem_limit_bytes=32 << 20),
        cost_estimate=pl.CostEstimate(flops=0, bytes_accessed=12_000_000, transcendentals=0),
    )(planes)


def conv_kernel(ids_ref, x_ref, *refs, rows, width):
    pieces, (send_ref, keep_ref, stats_ref, w_ref, sum_ref, sems) = refs[:8], refs[8:]
    core, colour = ids_ref[0], ids_ref[1]
    j = pl.program_id(0)
    outs = keep_ref.shape[2]

    @pl.when(j == 0)
    def _():
        copies = []
        for s in range(4):
            for h in range(2):
                dst = w_ref.at[s, :, h * outs // 2 : (h + 1) * outs // 2, :]
                copies.append(pltpu.make_async_copy(pieces[2 * s + h], dst, sems.at[2 * s + h]))
        for copy in copies:
            copy.start()
        for copy in copies:
            copy.wait()
        sum_ref[...] = jnp.zeros_like(sum_ref)

    plane = (j + 2 * (1 - core)) % 4
    total = None
    for a in range(3):
        taps = [(quarter_of(t), t - QUARTER_START[quarter_of(t)]) for t in range(9 * a, 9 * a + 9)]
        rhs = jnp.concatenate([w_ref[jnp.bitwise_xor(colour, q), i] for q, i in taps], axis=1)
        lhs = jnp.concatenate([x_ref[plane + a, b * width : b * width + rows, :] for b in range(3)], axis=1)
        part = lax.dot_general(lhs, rhs, (((1,), (1,)), ((), ())), preferred_element_type=jnp.float32)
        total = part if total is None else total + part
    sum_ref[0:1, :] += jnp.sum(total, axis=0, keepdims=True)
    sum_ref[1:2, :] += jnp.sum(total * total, axis=0, keepdims=True)

    @pl.when(j < 2)
    def _():
        send_ref[0, :, 0:outs] = total
        send_ref[0, :, outs:] = jnp.zeros((rows, send_ref.shape[2] - outs), jnp.float32)

    @pl.when(j >= 2)
    def _():
        keep_ref[0] = total

    @pl.when(j == 3)
    def _():
        row = jnp.concatenate([sum_ref[0:1, :], sum_ref[1:2, :]], axis=1)
        stats_ref[...] = jnp.broadcast_to(row, stats_ref.shape)


def conv(ids, wide, pieces, rows, width, group):
    taps, half, chans = pieces[0].shape
    outs = 2 * half
    spec = pltpu.PrefetchScalarGridSpec(
        num_scalar_prefetch=1,
        grid=(4,),
        in_specs=[pl.BlockSpec(memory_space=pltpu.VMEM)] + [pl.BlockSpec(memory_space=pl.ANY)] * 8,
        out_specs=[
            pl.BlockSpec((1, rows, PADDED), lambda j, ids: (jnp.minimum(j, 1), 0, 0)),
            pl.BlockSpec((1, rows, outs), lambda j, ids: (jnp.maximum(j - 2, 0), 0, 0)),
            pl.BlockSpec((group, 2 * outs), lambda j, ids: (0, 0)),
        ],
        scratch_shapes=[
            pltpu.VMEM((4, taps, outs, chans), jnp.bfloat16),
            pltpu.VMEM((8, outs), jnp.float32),
            pltpu.SemaphoreType.DMA((8,)),
        ],
    )
    return pl.pallas_call(
        functools.partial(conv_kernel, rows=rows, width=width),
        grid_spec=spec,
        out_shape=[
            jax.ShapeDtypeStruct((2, rows, PADDED), jnp.float32),
            jax.ShapeDtypeStruct((2, rows, outs), jnp.float32),
            jax.ShapeDtypeStruct((group, 2 * outs), jnp.float32),
        ],
        compiler_params=pltpu.CompilerParams(vmem_limit_bytes=40 << 20),
        cost_estimate=pl.CostEstimate(flops=8 * 10**9, bytes_accessed=16_000_000, transcendentals=0),
    )(ids, wide, *pieces)


def norm_kernel(ids_ref, keep_ref, recv_ref, stats_ref, gain_ref, shift_ref, o_ref, *, cells):
    first = ids_ref[0] == 0
    outs = keep_ref.shape[2]
    keep, recv = keep_ref[0], recv_ref[0, :, 0:outs]
    for half in range(2):
        sums = stats_ref[half : half + 1, :]
        for chip in range(1, stats_ref.shape[0] // 2):
            sums = sums + stats_ref[2 * chip + half : 2 * chip + half + 1, :]
        mean = sums[:, 0:outs] / cells
        variance = sums[:, outs : 2 * outs] / cells - mean * mean
        scale = gain_ref[half] / jnp.sqrt(variance + EPS)
        conv_out = jnp.where(first, keep, recv) if half == 0 else jnp.where(first, recv, keep)
        normed = (conv_out - mean) * scale + shift_ref[half]
        active = jnp.where(normed >= 0, normed, 0.01 * normed).astype(o_ref.dtype)
        o_ref[0, :, half * outs : (half + 1) * outs] = active


def normalize(ids, keep, recv, stats, gain, shift, cells):
    planes, rows, outs = keep.shape
    tile = 256
    spec = pltpu.PrefetchScalarGridSpec(
        num_scalar_prefetch=1,
        grid=(planes, rows // tile),
        in_specs=[
            pl.BlockSpec((1, tile, outs), lambda i, j, ids: (i, j, 0)),
            pl.BlockSpec((1, tile, PADDED), lambda i, j, ids: (i, j, 0)),
            pl.BlockSpec(stats.shape, lambda i, j, ids: (0, 0)),
            pl.BlockSpec((2, 1, outs), lambda i, j, ids: (0, 0, 0)),
            pl.BlockSpec((2, 1, outs), lambda i, j, ids: (0, 0, 0)),
        ],
        out_specs=pl.BlockSpec((1, tile, 2 * outs), lambda i, j, ids: (i, j, 0)),
    )
    return pl.pallas_call(
        functools.partial(norm_kernel, cells=cells),
        grid_spec=spec,
        out_shape=jax.ShapeDtypeStruct((planes, rows, 2 * outs), jnp.bfloat16),
        compiler_params=pltpu.CompilerParams(vmem_limit_bytes=32 << 20),
        cost_estimate=pl.CostEstimate(flops=4_000_000, bytes_accessed=3_000_000, transcendentals=0),
    )(ids, keep, recv, stats, gain, shift)


def join_kernel(ids_ref, *refs):
    pieces, (low_ref, high_ref, sems) = refs[:8], refs[8:]
    step = pieces[0].shape[1]
    z = ids_ref[2]
    for r in range(8):
        where = jnp.remainder(z - r + 8, 8)
        rows = pl.ds(pl.multiple_of(jnp.remainder(where, 4) * step, 8), step)

        @pl.when(where < 4)
        def _():
            pltpu.make_async_copy(pieces[r], low_ref.at[:, rows, :], sems.at[r]).start()

        @pl.when(where >= 4)
        def _():
            pltpu.make_async_copy(pieces[r], high_ref.at[:, rows, :], sems.at[r]).start()

    for r in range(8):
        pltpu.make_async_copy(pieces[r], low_ref.at[:, pl.ds(0, step), :], sems.at[r]).wait()


def join(ids, pieces):
    taps, step, chans = pieces[0].shape
    part = jax.ShapeDtypeStruct((taps, 4 * step, chans), jnp.bfloat16)
    spec = pltpu.PrefetchScalarGridSpec(
        num_scalar_prefetch=1,
        grid=(),
        in_specs=[pl.BlockSpec(memory_space=pl.ANY)] * 8,
        out_specs=[pl.BlockSpec(memory_space=pl.ANY)] * 2,
        scratch_shapes=[pltpu.SemaphoreType.DMA((8,))],
    )
    return pl.pallas_call(
        join_kernel,
        grid_spec=spec,
        out_shape=[part, part],
        cost_estimate=pl.CostEstimate(flops=0, bytes_accessed=2_000_000, transcendentals=0),
    )(ids, *pieces)


def chip_planes(slab, core):
    other = lax.ppermute(slab, "c", SWAP)
    inner = jnp.where(core == 0, jnp.concatenate([slab, other]), jnp.concatenate([other, slab]))
    chips = SIZES[2] * SIZES[3]
    before = lax.ppermute(inner[3:], CHIPS, [(i, i + 1) for i in range(chips - 1)])
    after = lax.ppermute(inner[:1], CHIPS, [(i + 1, i) for i in range(chips - 1)])
    return jnp.concatenate([before, inner, after])


def gather_quarter(shard, core, ids):
    xh, z, y, xl = (lax.axis_index(n) for n in ("xh", "z", "y", "xl"))
    to_xl = jnp.where(core == xh, xl, 1 - xl)
    parts = []
    for odd in range(2):
        colour = 2 * ((y + to_xl) % 2) + (z + odd + to_xl) % 2
        parts.append(lax.dynamic_slice_in_dim(shard, jnp.minimum(7 * colour, 20), 7, axis=0))
    pieces = []
    for r in range(8):
        perm = []
        for here_z in range(8):
            there_z = (here_z + r) % 8
            for h in range(2):
                for x_low in range(2):
                    for c in range(2):
                        src = ((h * 8 + here_z) * 2 + x_low) * 2 + c
                        if c == h:
                            dst = ((h * 8 + there_z) * 2 + x_low) * 2 + c
                        else:
                            dst = (((1 - h) * 8 + there_z) * 2 + 1 - x_low) * 2 + h
                        perm.append((src, dst))
        pieces.append(lax.ppermute(parts[r % 2], ("xh", "z", "xl", "c"), perm))
    return join(ids, pieces)


def ring(array, axes, by):
    count = math.prod(SIZES[AXES.index(n)] for n in axes)
    return lax.ppermute(array, axes, [(i, (i + by) % count) for i in range(count)])


def gather_weights(shard, core, ids):
    low, high = gather_quarter(shard, core, ids)
    pieces = [low, high]
    for axes in (("z",), ("y",), ("xh", "xl")):
        pieces += [ring(low, axes, 1), ring(high, axes, -1)]
    return pieces


def local(slabs, kernel, gain, shift):
    core = lax.axis_index("c")
    z, y, xl = (lax.axis_index(n) for n in ("z", "y", "xl"))
    colour = 2 * ((y + xl) % 2) + (z + xl) % 2
    ids = jnp.stack([core, colour, z]).astype(jnp.int32)
    _, planes, height, width, chans = slabs.shape
    rows = height * width
    outs = chans // 2
    group = SIZES[2] * SIZES[3] * SIZES[4]

    shard = jnp.transpose(kernel, (0, 1, 2, 4, 3)).reshape(27, kernel.shape[4], chans)
    pieces = gather_weights(shard, core, ids)
    wide = widen(chip_planes(slabs[0].reshape(planes, rows, chans), core), width)
    send, keep, stats = conv(ids, wide, pieces, rows, width, group)

    recv = lax.ppermute(send, "c", SWAP)
    everyone = lax.all_to_all(stats, DEPTH, 0, 0, tiled=True)
    cells = planes * rows * group
    out = normalize(
        ids, keep, recv, everyone, gain.reshape(2, 1, outs), shift.reshape(2, 1, outs), cells
    )
    return out.reshape(slabs.shape)


def solution(mesh):
    fine = Mesh(mesh.devices.reshape(SIZES), AXES)
    x_spec = P(("xh", "z"), DEPTH, None, None, None)
    in_specs = (x_spec, P(None, None, None, None, ("xh", "z")), P(), P())
    return jax.shard_map(local, mesh=fine, in_specs=in_specs, out_specs=x_spec, check_vma=False)
```

```python
import functools
import math

import jax
import jax.numpy as jnp
from jax import lax
from jax.experimental import pallas as pl
from jax.experimental.pallas import tpu as pltpu
from jax.sharding import Mesh, PartitionSpec as P

AXES = ("xh", "z", "y", "xl", "c")
SIZES = (2, 8, 4, 2, 2)
CHIPS = ("y", "xl")
DEPTH = ("y", "xl", "c")
SWAP = [(0, 1), (1, 0)]
EPS = 1e-05
PADDED = 256

def shift_rows(plane, by, width):
    rows = plane.shape[0]
    moved = pltpu.roll(plane, by % rows, 0)
    w = lax.broadcasted_iota(jnp.int32, plane.shape, 0) % width
    edge = 0 if by == 1 else width - 1
    return jnp.where(w == edge, 0.0, moved)


def widen_kernel(x_ref, o_ref, *, width):
    x = x_ref[0]
    rows, chans = x.shape
    zero = jnp.zeros((width, 3 * chans), o_ref.dtype)
    o_ref[0, 0:width, :] = zero
    o_ref[0, width + rows : 2 * width + rows, :] = zero
    wide = x.astype(jnp.float32)
    o_ref[0, width : width + rows, 0:chans] = shift_rows(wide, 1, width).astype(o_ref.dtype)
    o_ref[0, width : width + rows, chans : 2 * chans] = x
    o_ref[0, width : width + rows, 2 * chans : 3 * chans] = shift_rows(wide, -1, width).astype(o_ref.dtype)


def widen(planes, width):
    count, rows, chans = planes.shape
    return pl.pallas_call(
        functools.partial(widen_kernel, width=width),
        grid=(count,),
        in_specs=[pl.BlockSpec((1, rows, chans), lambda i: (i, 0, 0))],
        out_specs=pl.BlockSpec((1, rows + 2 * width, 3 * chans), lambda i: (i, 0, 0)),
        out_shape=jax.ShapeDtypeStruct((count, rows + 2 * width, 3 * chans), planes.dtype),
        compiler_params=pltpu.CompilerParams(vmem_limit_bytes=32 << 20),
        cost_estimate=pl.CostEstimate(flops=0, bytes_accessed=12_000_000, transcendentals=0),
    )(planes)


def half_conv(x_ref, w_ref, plane, taps, rows, width):
    chans = w_ref.shape[2]
    lhs, rhs = [], []
    for i, t in taps:
        a, b, e = t // 9, t // 3 % 3, t % 3
        lhs.append(x_ref[plane + a, b * width : b * width + rows, e * chans : (e + 1) * chans])
        rhs.append(w_ref[i])
    lhs, rhs = jnp.concatenate(lhs, axis=1), jnp.concatenate(rhs, axis=1)
    return lax.dot_general(lhs, rhs, (((1,), (1,)), ((), ())), preferred_element_type=jnp.float32)


LOW_TAPS = [(t, t) for t in range(14)]
HIGH_TAPS = [(t - 13, t) for t in range(14, 27)]


def first_kernel(ids_ref, x_ref, w_ref, acc_ref, *, rows, width):
    core, colour = ids_ref[0], ids_ref[1]
    j = pl.program_id(0)
    plane = (j + 2 * (1 - core)) % 4

    @pl.when(colour == 0)
    def _():
        acc_ref[0] = half_conv(x_ref, w_ref, plane, LOW_TAPS, rows, width)

    @pl.when(colour != 0)
    def _():
        acc_ref[0] = half_conv(x_ref, w_ref, plane, HIGH_TAPS, rows, width)


def second_kernel(ids_ref, x_ref, w_ref, acc_ref, before_ref, out_ref, stats_ref, total_ref, sum_ref, *, rows, width, keep):
    core, colour = ids_ref[0], ids_ref[1]
    j = pl.program_id(0)
    outs = total_ref.shape[1]

    @pl.when(j == 0)
    def _():
        sum_ref[...] = before_ref[...] if keep else jnp.zeros_like(sum_ref)

    plane = (j + 2 * keep + 2 * (1 - core)) % 4

    @pl.when(colour == 0)
    def _():
        total_ref[...] = acc_ref[0] + half_conv(x_ref, w_ref, plane, HIGH_TAPS, rows, width)

    @pl.when(colour != 0)
    def _():
        total_ref[...] = acc_ref[0] + half_conv(x_ref, w_ref, plane, LOW_TAPS, rows, width)

    total = total_ref[...]
    sum_ref[0:1, :] += jnp.sum(total, axis=0, keepdims=True)
    sum_ref[1:2, :] += jnp.sum(total * total, axis=0, keepdims=True)
    out_ref[0, :, 0:outs] = total
    if not keep:
        out_ref[0, :, outs:] = jnp.zeros((rows, out_ref.shape[2] - outs), jnp.float32)

    @pl.when(j == 1)
    def _():
        if keep:
            row = jnp.concatenate([sum_ref[0:1, :], sum_ref[1:2, :]], axis=1)
            stats_ref[...] = jnp.broadcast_to(row[None], stats_ref.shape)
        else:
            stats_ref[...] = sum_ref[...]


def first_conv(ids, wide, own, rows, width):
    outs = own.shape[1]
    whole = pl.BlockSpec(memory_space=pltpu.VMEM)
    return pl.pallas_call(
        functools.partial(first_kernel, rows=rows, width=width),
        grid_spec=pltpu.PrefetchScalarGridSpec(
            num_scalar_prefetch=1,
            grid=(4,),
            in_specs=[whole, whole],
            out_specs=pl.BlockSpec((1, rows, outs), lambda j, ids: (j, 0, 0)),
        ),
        out_shape=jax.ShapeDtypeStruct((4, rows, outs), jnp.float32),
        compiler_params=pltpu.CompilerParams(vmem_limit_bytes=40 << 20),
        cost_estimate=pl.CostEstimate(flops=5 * 10**9, bytes_accessed=12_000_000, transcendentals=0),
    )(ids, wide, own)


def second_conv(ids, wide, other, acc, before, rows, width, group, keep):
    outs = other.shape[1]
    lanes = outs if keep else PADDED
    stats = (group, 1, 2 * outs) if keep else (8, outs)
    whole = pl.BlockSpec(memory_space=pltpu.VMEM)
    return pl.pallas_call(
        functools.partial(second_kernel, rows=rows, width=width, keep=keep),
        grid_spec=pltpu.PrefetchScalarGridSpec(
            num_scalar_prefetch=1,
            grid=(2,),
            in_specs=[whole, whole, pl.BlockSpec((1, rows, outs), lambda j, ids: (j + 2 * keep, 0, 0)), whole],
            out_specs=[
                pl.BlockSpec((1, rows, lanes), lambda j, ids: (j, 0, 0)),
                pl.BlockSpec(stats, lambda j, ids: (0,) * len(stats)),
            ],
            scratch_shapes=[pltpu.VMEM((rows, outs), jnp.float32), pltpu.VMEM((8, outs), jnp.float32)],
        ),
        out_shape=[jax.ShapeDtypeStruct((2, rows, lanes), jnp.float32), jax.ShapeDtypeStruct(stats, jnp.float32)],
        compiler_params=pltpu.CompilerParams(vmem_limit_bytes=40 << 20),
        cost_estimate=pl.CostEstimate(flops=2 * 10**9, bytes_accessed=8_000_000, transcendentals=0),
    )(ids, wide, other, acc, before)


def norm_kernel(ids_ref, keep_ref, recv_ref, stats_ref, gain_ref, shift_ref, o_ref, *, cells):
    first = ids_ref[0] == 0
    outs = keep_ref.shape[2]
    keep, recv = keep_ref[0], recv_ref[0, :, 0:outs]
    for half in range(2):
        sums = stats_ref[half]
        for chip in range(1, stats_ref.shape[0] // 2):
            sums = sums + stats_ref[2 * chip + half]
        mean = sums[:, 0:outs] / cells
        variance = sums[:, outs : 2 * outs] / cells - mean * mean
        scale = gain_ref[half] / jnp.sqrt(variance + EPS)
        conv_out = jnp.where(first, keep, recv) if half == 0 else jnp.where(first, recv, keep)
        normed = (conv_out - mean) * scale + shift_ref[half]
        active = jnp.where(normed >= 0, normed, 0.01 * normed).astype(o_ref.dtype)
        o_ref[0, :, half * outs : (half + 1) * outs] = active


def normalize(ids, keep, recv, stats, gain, shift, cells):
    planes, rows, outs = keep.shape
    tile = 256
    spec = pltpu.PrefetchScalarGridSpec(
        num_scalar_prefetch=1,
        grid=(planes, rows // tile),
        in_specs=[
            pl.BlockSpec((1, tile, outs), lambda i, j, ids: (i, j, 0)),
            pl.BlockSpec((1, tile, PADDED), lambda i, j, ids: (i, j, 0)),
            pl.BlockSpec(stats.shape, lambda i, j, ids: (0, 0, 0)),
            pl.BlockSpec((2, 1, outs), lambda i, j, ids: (0, 0, 0)),
            pl.BlockSpec((2, 1, outs), lambda i, j, ids: (0, 0, 0)),
        ],
        out_specs=pl.BlockSpec((1, tile, 2 * outs), lambda i, j, ids: (i, j, 0)),
    )
    return pl.pallas_call(
        functools.partial(norm_kernel, cells=cells),
        grid_spec=spec,
        out_shape=jax.ShapeDtypeStruct((planes, rows, 2 * outs), jnp.bfloat16),
        compiler_params=pltpu.CompilerParams(vmem_limit_bytes=32 << 20),
        cost_estimate=pl.CostEstimate(flops=4_000_000, bytes_accessed=3_000_000, transcendentals=0),
    )(ids, keep, recv, stats, gain, shift)


def chip_planes(slab, core):
    count = SIZES[2] * SIZES[3] * SIZES[4]
    pairs = []
    for d in range(count):
        to = d + 1 if d % 2 else d - 1
        if 0 <= to < count:
            pairs.append((d, to))
    edge = lax.dynamic_slice_in_dim(slab, core, 1, axis=0)
    halo = lax.ppermute(edge, DEPTH, pairs)
    mine = jnp.concatenate([halo, slab])
    other = lax.ppermute(mine, "c", SWAP)
    low = jnp.concatenate([mine, other[1:], other[:1]])
    high = jnp.concatenate([other, slab, halo])
    return jnp.where(core == 0, low, high)


def from_z(array, r):
    perm = []
    for here in range(8):
        there = (here + r) % 8
        for h in range(2):
            for xl in range(2):
                for c in range(2):
                    src = ((h * 8 + here) * 2 + xl) * 2 + c
                    if c == h:
                        dst = ((h * 8 + there) * 2 + xl) * 2 + c
                    else:
                        dst = (((1 - h) * 8 + there) * 2 + 1 - xl) * 2 + h
                    perm.append((src, dst))
    return lax.ppermute(array, ("xh", "z", "xl", "c"), perm)


def ring(array, axes, by):
    count = math.prod(SIZES[AXES.index(n)] for n in axes)
    return lax.ppermute(array, axes, [(i, (i + by) % count) for i in range(count)])


def put(buffer, piece, z, r, tap=0):
    where = jnp.remainder(z - r + 8, 8)
    return lax.dynamic_update_slice(buffer, piece[:, None], (tap, where, 0, 0))


def gather_weights(shard, core):
    xh, zi, y, xl = (lax.axis_index(n) for n in ("xh", "z", "y", "xl"))
    to_xl = jnp.where(core == xh, xl, 1 - xl)
    part = lax.dynamic_slice_in_dim(shard, 13 * ((y + to_xl) % 2), 14, axis=0)
    xs, ys, zs = ("xh", "xl"), ("y",), ("z",)
    up, down, here = from_z(part, 1), from_z(part, -1), from_z(part, 0)
    up2, down2 = ring(up, zs, 1), ring(down, zs, -1)
    far_up, far_down = ring(jnp.stack([here, up, up2]), xs, 1), ring(jnp.stack([down, down2]), xs, -1)
    up3, down3 = ring(up2, zs, 1), ring(down2, zs, -1)
    top, bottom = ring(up3[:7], zs, 1), ring(down3[7:], zs, -1)
    far_top = ring(jnp.concatenate([up3, top]), ys, 1)
    far_bottom = ring(jnp.concatenate([down3, bottom]), ys, -1)

    own = jnp.zeros((14, 8) + shard.shape[1:], shard.dtype)
    for r, piece in ((0, here), (1, up), (-1, down), (2, up2), (-2, down2), (3, up3), (-3, down3)):
        own = put(own, piece, zi, r)
    own = put(put(own, top, zi, 4), bottom, zi, 4, 7)
    other = jnp.zeros_like(own)
    for n in range(3):
        other = put(other, far_up[n], zi, n)
    for n in range(2):
        other = put(other, far_down[n], zi, -n - 1)
    merged = (14, 8 * shard.shape[1], shard.shape[2])

    def finish(gate):
        low, high, _ = lax.optimization_barrier((far_top, far_bottom, gate))
        full = put(put(other, low[:14], zi, 3), high[:14], zi, -3)
        full = put(put(full, low[14:], zi, 4), high[14:], zi, 4, 7)
        return full.reshape(merged)

    return own.reshape(merged), finish, up


def local(slabs, kernel, gain, shift):
    core = lax.axis_index("c")
    z, y, xl = (lax.axis_index(n) for n in ("z", "y", "xl"))
    colour = (y + xl) % 2
    ids = jnp.stack([core, colour, z]).astype(jnp.int32)
    _, planes, height, width, chans = slabs.shape
    rows = height * width
    outs = chans // 2
    group = SIZES[2] * SIZES[3] * SIZES[4]

    shard = jnp.transpose(kernel, (0, 1, 2, 4, 3)).reshape(27, kernel.shape[4], chans)
    own, finish, first = gather_weights(shard, core)
    slab, _ = lax.optimization_barrier((slabs[0].reshape(planes, rows, chans), first))
    wide = widen(chip_planes(slab, core), width)
    acc = first_conv(ids, wide, own, rows, width)
    other = finish(acc)
    send, sums = second_conv(ids, wide, other, acc, jnp.zeros((8, outs), jnp.float32), rows, width, group, 0)
    recv = lax.ppermute(send, "c", SWAP)
    keep, stats = second_conv(ids, wide, other, acc, sums, rows, width, group, 1)
    everyone = lax.all_to_all(stats, DEPTH, 0, 0, tiled=True)
    cells = planes * rows * group
    out = normalize(
        ids, keep, recv, everyone, gain.reshape(2, 1, outs), shift.reshape(2, 1, outs), cells
    )
    return out.reshape(slabs.shape)


def solution(mesh):
    fine = Mesh(mesh.devices.reshape(SIZES), AXES)
    x_spec = P(("xh", "z"), DEPTH, None, None, None)
    in_specs = (x_spec, P(None, None, None, None, ("xh", "z")), P(), P())
    return jax.shard_map(local, mesh=fine, in_specs=in_specs, out_specs=x_spec, check_vma=False)
```

```python
import functools
import math

import jax
import jax.numpy as jnp
from jax import lax
from jax.experimental import pallas as pl
from jax.experimental.pallas import tpu as pltpu
from jax.sharding import Mesh, PartitionSpec as P

AXES = ("xh", "z", "y", "xl", "c")
SIZES = (2, 8, 4, 2, 2)
CHIPS = ("y", "xl")
DEPTH = ("y", "xl", "c")
SWAP = [(0, 1), (1, 0)]
EPS = 1e-05
PADDED = 256

def shift_rows(plane, by, width):
    rows = plane.shape[0]
    moved = pltpu.roll(plane, by % rows, 0)
    w = lax.broadcasted_iota(jnp.int32, plane.shape, 0) % width
    edge = 0 if by == 1 else width - 1
    return jnp.where(w == edge, 0.0, moved)


def widen_kernel(x_ref, o_ref, *, width):
    x = x_ref[0]
    rows, chans = x.shape
    zero = jnp.zeros((width, 3 * chans), o_ref.dtype)
    o_ref[0, 0:width, :] = zero
    o_ref[0, width + rows : 2 * width + rows, :] = zero
    wide = x.astype(jnp.float32)
    o_ref[0, width : width + rows, 0:chans] = shift_rows(wide, 1, width).astype(o_ref.dtype)
    o_ref[0, width : width + rows, chans : 2 * chans] = x
    o_ref[0, width : width + rows, 2 * chans : 3 * chans] = shift_rows(wide, -1, width).astype(o_ref.dtype)


def widen(planes, width):
    count, rows, chans = planes.shape
    return pl.pallas_call(
        functools.partial(widen_kernel, width=width),
        grid=(count,),
        in_specs=[pl.BlockSpec((1, rows, chans), lambda i: (i, 0, 0))],
        out_specs=pl.BlockSpec((1, rows + 2 * width, 3 * chans), lambda i: (i, 0, 0)),
        out_shape=jax.ShapeDtypeStruct((count, rows + 2 * width, 3 * chans), planes.dtype),
        compiler_params=pltpu.CompilerParams(vmem_limit_bytes=32 << 20),
        cost_estimate=pl.CostEstimate(flops=0, bytes_accessed=12_000_000, transcendentals=0),
    )(planes)


def half_conv(x_ref, w_ref, plane, taps, rows, width):
    chans = w_ref.shape[2]
    lhs, rhs = [], []
    for i, t in taps:
        a, b, e = t // 9, t // 3 % 3, t % 3
        lhs.append(x_ref[plane + a, b * width : b * width + rows, e * chans : (e + 1) * chans])
        rhs.append(w_ref[i])
    lhs, rhs = jnp.concatenate(lhs, axis=1), jnp.concatenate(rhs, axis=1)
    return lax.dot_general(lhs, rhs, (((1,), (1,)), ((), ())), preferred_element_type=jnp.float32)


LOW_TAPS = [(t, t) for t in range(14)]
HIGH_TAPS = [(t - 13, t) for t in range(14, 27)]


def first_kernel(ids_ref, x_ref, w_ref, acc_ref, *, rows, width):
    core, colour = ids_ref[0], ids_ref[1]

    def run(taps):
        for j in range(4):
            plane = (j + 2 * (1 - core)) % 4
            acc_ref[j] = half_conv(x_ref, w_ref, plane, taps, rows, width)

    pl.when(colour == 0)(lambda: run(LOW_TAPS))
    pl.when(colour != 0)(lambda: run(HIGH_TAPS))


def second_kernel(ids_ref, x_ref, w_ref, acc_ref, before_ref, out_ref, stats_ref, sum_ref, *, rows, width, keep):
    core, colour = ids_ref[0], ids_ref[1]
    outs = acc_ref.shape[2]
    sum_ref[...] = before_ref[...] if keep else jnp.zeros_like(sum_ref)

    def run(taps):
        for j in range(2):
            plane = (j + 2 * keep + 2 * (1 - core)) % 4
            total = acc_ref[j + 2 * keep] + half_conv(x_ref, w_ref, plane, taps, rows, width)
            sum_ref[0:1, :] += jnp.sum(total, axis=0, keepdims=True)
            sum_ref[1:2, :] += jnp.sum(total * total, axis=0, keepdims=True)
            out_ref[j, :, 0:outs] = total
            if not keep:
                out_ref[j, :, outs:] = jnp.zeros((rows, out_ref.shape[2] - outs), jnp.float32)

    pl.when(colour == 0)(lambda: run(HIGH_TAPS))
    pl.when(colour != 0)(lambda: run(LOW_TAPS))
    if keep:
        row = jnp.concatenate([sum_ref[0:1, :], sum_ref[1:2, :]], axis=1)
        stats_ref[...] = jnp.broadcast_to(row[None], stats_ref.shape)
    else:
        stats_ref[...] = sum_ref[...]


def in_vmem(kernel, count, out_shape, scratch, flops, limit):
    whole = pl.BlockSpec(memory_space=pltpu.VMEM)
    outs = [whole] * len(out_shape)
    return pl.pallas_call(
        kernel,
        grid_spec=pltpu.PrefetchScalarGridSpec(
            num_scalar_prefetch=1, grid=(), in_specs=[whole] * count, out_specs=outs, scratch_shapes=scratch
        ),
        out_shape=out_shape,
        compiler_params=pltpu.CompilerParams(vmem_limit_bytes=limit << 20),
        cost_estimate=pl.CostEstimate(flops=flops, bytes_accessed=8_000_000, transcendentals=0),
    )


def first_conv(ids, wide, own, rows, width):
    kernel = functools.partial(first_kernel, rows=rows, width=width)
    out = [jax.ShapeDtypeStruct((4, rows, own.shape[1]), jnp.float32)]
    return in_vmem(kernel, 2, out, [], 5 * 10**9, 40)(ids, wide, own)[0]


def second_conv(ids, wide, other, acc, before, rows, width, group, keep):
    outs = other.shape[1]
    lanes = outs if keep else PADDED
    stats = (group, 1, 2 * outs) if keep else (8, outs)
    kernel = functools.partial(second_kernel, rows=rows, width=width, keep=keep)
    out = [jax.ShapeDtypeStruct((2, rows, lanes), jnp.float32), jax.ShapeDtypeStruct(stats, jnp.float32)]
    scratch = [pltpu.VMEM((8, outs), jnp.float32)]
    return in_vmem(kernel, 4, out, scratch, 2 * 10**9, 40)(ids, wide, other, acc, before)


def norm_kernel(ids_ref, keep_ref, recv_ref, stats_ref, gain_ref, shift_ref, o_ref, mean_ref, scale_ref, *, cells):
    first = ids_ref[0] == 0
    outs = keep_ref.shape[2]
    plane, tile = pl.program_id(0), o_ref.shape[1]

    @pl.when((plane == 0) & (pl.program_id(1) == 0))
    def _():
        for half in range(2):
            sums = stats_ref[half]
            for chip in range(1, stats_ref.shape[0] // 2):
                sums = sums + stats_ref[2 * chip + half]
            mean = sums[:, 0:outs] / cells
            variance = sums[:, outs : 2 * outs] / cells - mean * mean
            mean_ref[half] = mean
            scale_ref[half] = gain_ref[half] / jnp.sqrt(variance + EPS)

    where = pl.ds(pl.multiple_of(pl.program_id(1) * tile, tile), tile)
    keep, recv = keep_ref[plane, where, :], recv_ref[plane, where, 0:outs]
    for half in range(2):
        conv_out = jnp.where(first, keep, recv) if half == 0 else jnp.where(first, recv, keep)
        normed = (conv_out - mean_ref[half]) * scale_ref[half] + shift_ref[half]
        active = jnp.where(normed >= 0, normed, 0.01 * normed).astype(o_ref.dtype)
        o_ref[0, :, half * outs : (half + 1) * outs] = active


def normalize(ids, keep, recv, stats, gain, shift, cells):
    planes, rows, outs = keep.shape
    tile = 256
    spec = pltpu.PrefetchScalarGridSpec(
        num_scalar_prefetch=1,
        grid=(planes, rows // tile),
        in_specs=[pl.BlockSpec(memory_space=pltpu.VMEM)] * 5,
        out_specs=pl.BlockSpec((1, tile, 2 * outs), lambda i, j, ids: (i, j, 0)),
        scratch_shapes=[pltpu.VMEM((2, 1, outs), jnp.float32)] * 2,
    )
    return pl.pallas_call(
        functools.partial(norm_kernel, cells=cells),
        grid_spec=spec,
        out_shape=jax.ShapeDtypeStruct((planes, rows, 2 * outs), jnp.bfloat16),
        compiler_params=pltpu.CompilerParams(vmem_limit_bytes=32 << 20),
        cost_estimate=pl.CostEstimate(flops=4_000_000, bytes_accessed=3_000_000, transcendentals=0),
    )(ids, keep, recv, stats, gain, shift)


def chip_planes(slab, core):
    count = SIZES[2] * SIZES[3] * SIZES[4]
    pairs = []
    for d in range(count):
        to = d + 1 if d % 2 else d - 1
        if 0 <= to < count:
            pairs.append((d, to))
    edge = lax.dynamic_slice_in_dim(slab, core, 1, axis=0)
    halo = lax.ppermute(edge, DEPTH, pairs)
    mine = jnp.concatenate([halo, slab])
    other = lax.ppermute(mine, "c", SWAP)
    low = jnp.concatenate([mine, other[1:], other[:1]])
    high = jnp.concatenate([other, slab, halo])
    return jnp.where(core == 0, low, high)


def from_z(array, r):
    perm = []
    for here in range(8):
        there = (here + r) % 8
        for h in range(2):
            for xl in range(2):
                for c in range(2):
                    src = ((h * 8 + here) * 2 + xl) * 2 + c
                    if c == h:
                        dst = ((h * 8 + there) * 2 + xl) * 2 + c
                    else:
                        dst = (((1 - h) * 8 + there) * 2 + 1 - xl) * 2 + h
                    perm.append((src, dst))
    return lax.ppermute(array, ("xh", "z", "xl", "c"), perm)


def ring(array, axes, by):
    count = math.prod(SIZES[AXES.index(n)] for n in axes)
    return lax.ppermute(array, axes, [(i, (i + by) % count) for i in range(count)])


def put(buffer, piece, z, r, tap=0):
    where = jnp.remainder(z - r + 8, 8)
    return lax.dynamic_update_slice(buffer, piece[:, None], (tap, where, 0, 0))


def gather_weights(shard, core, widened):
    xh, zi, y, xl = (lax.axis_index(n) for n in ("xh", "z", "y", "xl"))
    to_xl = jnp.where(core == xh, xl, 1 - xl)
    part = lax.dynamic_slice_in_dim(shard, 13 * ((y + to_xl) % 2), 14, axis=0)
    xs, ys, zs = ("xh", "xl"), ("y",), ("z",)
    up, down, here = from_z(part, 1), from_z(part, -1), from_z(part, 0)
    up2, down2 = ring(up, zs, 1), ring(down, zs, -1)
    far_up, far_down = ring(jnp.stack([here, up, up2]), xs, 1), ring(jnp.stack([down, down2]), xs, -1)
    up3, down3 = ring(up2, zs, 1), ring(down2, zs, -1)
    top, bottom = ring(up3[:7], zs, 1), ring(down3[7:], zs, -1)
    wide = widened()
    top, bottom, wide = lax.optimization_barrier((top, bottom, wide))
    far_top = ring(jnp.concatenate([up3, top]), ys, 1)
    far_bottom = ring(jnp.concatenate([down3, bottom]), ys, -1)

    own = jnp.zeros((14, 8) + shard.shape[1:], shard.dtype)
    for r, piece in ((0, here), (1, up), (-1, down), (2, up2), (-2, down2), (3, up3), (-3, down3)):
        own = put(own, piece, zi, r)
    own = put(put(own, top, zi, 4), bottom, zi, 4, 7)
    merged = (14, 8 * shard.shape[1], shard.shape[2])

    def finish(gate):
        ups, downs, low, high, _ = lax.optimization_barrier((far_up, far_down, far_top, far_bottom, gate))
        other = jnp.zeros_like(own)
        for n in range(3):
            other = put(other, ups[n], zi, n)
        for n in range(2):
            other = put(other, downs[n], zi, -n - 1)
        other = put(put(other, low[:14], zi, 3), high[:14], zi, -3)
        other = put(put(other, low[14:], zi, 4), high[14:], zi, 4, 7)
        return other.reshape(merged)

    return own.reshape(merged), finish, wide


def local(slabs, kernel, gain, shift):
    core = lax.axis_index("c")
    z, y, xl = (lax.axis_index(n) for n in ("z", "y", "xl"))
    colour = (y + xl) % 2
    ids = jnp.stack([core, colour, z]).astype(jnp.int32)
    _, planes, height, width, chans = slabs.shape
    rows = height * width
    outs = chans // 2
    group = SIZES[2] * SIZES[3] * SIZES[4]

    shard = jnp.transpose(kernel, (0, 1, 2, 4, 3)).reshape(27, kernel.shape[4], chans)
    def widened():
        return widen(chip_planes(slabs[0].reshape(planes, rows, chans), core), width)

    own, finish, wide = gather_weights(shard, core, widened)
    acc = first_conv(ids, wide, own, rows, width)
    other = finish(acc)
    send, sums = second_conv(ids, wide, other, acc, jnp.zeros((8, outs), jnp.float32), rows, width, group, 0)
    recv = lax.ppermute(send, "c", SWAP)
    keep, stats = second_conv(ids, wide, other, acc, sums, rows, width, group, 1)
    everyone = lax.all_to_all(stats, DEPTH, 0, 0, tiled=True)
    cells = planes * rows * group
    out = normalize(
        ids, keep, recv, everyone, gain.reshape(2, 1, outs), shift.reshape(2, 1, outs), cells
    )
    return out.reshape(slabs.shape)


def solution(mesh):
    fine = Mesh(mesh.devices.reshape(SIZES), AXES)
    x_spec = P(("xh", "z"), DEPTH, None, None, None)
    in_specs = (x_spec, P(None, None, None, None, ("xh", "z")), P(), P())
    return jax.shard_map(local, mesh=fine, in_specs=in_specs, out_specs=x_spec, check_vma=False)
```

```python
import functools
import math

import jax
import jax.numpy as jnp
from jax import lax
from jax.experimental import pallas as pl
from jax.experimental.pallas import tpu as pltpu
from jax.sharding import Mesh, PartitionSpec as P

AXES = ("xh", "z", "y", "xl", "c")
SIZES = (2, 8, 4, 2, 2)
CHIPS = ("y", "xl")
DEPTH = ("y", "xl", "c")
SWAP = [(0, 1), (1, 0)]
EPS = 1e-05
PADDED = 256

def shift_rows(plane, by, width):
    rows = plane.shape[0]
    moved = pltpu.roll(plane, by % rows, 0)
    w = lax.broadcasted_iota(jnp.int32, plane.shape, 0) % width
    edge = 0 if by == 1 else width - 1
    return jnp.where(w == edge, 0.0, moved)


def widen_kernel(x_ref, o_ref, *, width):
    x = x_ref[0]
    rows, chans = x.shape
    zero = jnp.zeros((width, 3 * chans), o_ref.dtype)
    o_ref[0, 0:width, :] = zero
    o_ref[0, width + rows : 2 * width + rows, :] = zero
    wide = x.astype(jnp.float32)
    o_ref[0, width : width + rows, 0:chans] = shift_rows(wide, 1, width).astype(o_ref.dtype)
    o_ref[0, width : width + rows, chans : 2 * chans] = x
    o_ref[0, width : width + rows, 2 * chans : 3 * chans] = shift_rows(wide, -1, width).astype(o_ref.dtype)


def widen(planes, width):
    count, rows, chans = planes.shape
    return pl.pallas_call(
        functools.partial(widen_kernel, width=width),
        grid=(count,),
        in_specs=[pl.BlockSpec((1, rows, chans), lambda i: (i, 0, 0))],
        out_specs=pl.BlockSpec((1, rows + 2 * width, 3 * chans), lambda i: (i, 0, 0)),
        out_shape=jax.ShapeDtypeStruct((count, rows + 2 * width, 3 * chans), planes.dtype),
        compiler_params=pltpu.CompilerParams(vmem_limit_bytes=32 << 20),
        cost_estimate=pl.CostEstimate(flops=0, bytes_accessed=12_000_000, transcendentals=0),
    )(planes)


def half_conv(x_ref, w_ref, plane, taps, rows, width):
    chans = w_ref.shape[2]
    lhs, rhs = [], []
    for i, t in taps:
        a, b, e = t // 9, t // 3 % 3, t % 3
        lhs.append(x_ref[plane + a, b * width : b * width + rows, e * chans : (e + 1) * chans])
        rhs.append(w_ref[i])
    lhs, rhs = jnp.concatenate(lhs, axis=1), jnp.concatenate(rhs, axis=1)
    return lax.dot_general(lhs, rhs, (((1,), (1,)), ((), ())), preferred_element_type=jnp.float32)


LOW_TAPS = [(t, t) for t in range(14)]
HIGH_TAPS = [(t - 13, t) for t in range(14, 27)]


def first_kernel(ids_ref, x_ref, w_ref, acc_ref, *, rows, width):
    core, colour = ids_ref[0], ids_ref[1]

    def run(taps):
        for j in range(4):
            plane = (j + 2 * (1 - core)) % 4
            acc_ref[j] = half_conv(x_ref, w_ref, plane, taps, rows, width)

    pl.when(colour == 0)(lambda: run(LOW_TAPS))
    pl.when(colour != 0)(lambda: run(HIGH_TAPS))


def second_kernel(ids_ref, x_ref, w_ref, acc_ref, send_ref, keep_ref, stats_ref, sum_ref, *, rows, width):
    core, colour = ids_ref[0], ids_ref[1]
    outs = acc_ref.shape[2]
    sum_ref[...] = jnp.zeros_like(sum_ref)

    def run(taps):
        for j in range(4):
            plane = (j + 2 * (1 - core)) % 4
            total = acc_ref[j] + half_conv(x_ref, w_ref, plane, taps, rows, width)
            sum_ref[0:1, :] += jnp.sum(total, axis=0, keepdims=True)
            sum_ref[1:2, :] += jnp.sum(total * total, axis=0, keepdims=True)
            if j < 2:
                send_ref[j, :, 0:outs] = total
                send_ref[j, :, outs:] = jnp.zeros((rows, send_ref.shape[2] - outs), jnp.float32)
            else:
                keep_ref[j - 2] = total

    pl.when(colour == 0)(lambda: run(HIGH_TAPS))
    pl.when(colour != 0)(lambda: run(LOW_TAPS))
    row = jnp.concatenate([sum_ref[0:1, :], sum_ref[1:2, :]], axis=1)
    stats_ref[...] = jnp.broadcast_to(row[None], stats_ref.shape)


def in_vmem(kernel, count, out_shape, scratch, flops, limit):
    whole = pl.BlockSpec(memory_space=pltpu.VMEM)
    outs = [whole] * len(out_shape)
    return pl.pallas_call(
        kernel,
        grid_spec=pltpu.PrefetchScalarGridSpec(
            num_scalar_prefetch=1, grid=(), in_specs=[whole] * count, out_specs=outs, scratch_shapes=scratch
        ),
        out_shape=out_shape,
        compiler_params=pltpu.CompilerParams(vmem_limit_bytes=limit << 20),
        cost_estimate=pl.CostEstimate(flops=flops, bytes_accessed=8_000_000, transcendentals=0),
    )


def first_conv(ids, wide, own, rows, width):
    kernel = functools.partial(first_kernel, rows=rows, width=width)
    out = [jax.ShapeDtypeStruct((4, rows, own.shape[1]), jnp.float32)]
    return in_vmem(kernel, 2, out, [], 5 * 10**9, 40)(ids, wide, own)[0]


def second_conv(ids, wide, other, acc, rows, width, group):
    outs = other.shape[1]
    kernel = functools.partial(second_kernel, rows=rows, width=width)
    shapes = ((2, rows, PADDED), (2, rows, outs), (group, 1, 2 * outs))
    out = [jax.ShapeDtypeStruct(shape, jnp.float32) for shape in shapes]
    scratch = [pltpu.VMEM((8, outs), jnp.float32)]
    return in_vmem(kernel, 3, out, scratch, 5 * 10**9, 40)(ids, wide, other, acc)


def norm_kernel(ids_ref, keep_ref, recv_ref, stats_ref, gain_ref, shift_ref, o_ref, mean_ref, scale_ref, *, cells):
    first = ids_ref[0] == 0
    outs = keep_ref.shape[2]
    plane, tile = pl.program_id(0), o_ref.shape[1]

    @pl.when((plane == 0) & (pl.program_id(1) == 0))
    def _():
        for half in range(2):
            sums = stats_ref[half]
            for chip in range(1, stats_ref.shape[0] // 2):
                sums = sums + stats_ref[2 * chip + half]
            mean = sums[:, 0:outs] / cells
            variance = sums[:, outs : 2 * outs] / cells - mean * mean
            mean_ref[half] = mean
            scale_ref[half] = gain_ref[half] / jnp.sqrt(variance + EPS)

    where = pl.ds(pl.multiple_of(pl.program_id(1) * tile, tile), tile)
    keep, recv = keep_ref[plane, where, :], recv_ref[plane, where, 0:outs]
    for half in range(2):
        conv_out = jnp.where(first, keep, recv) if half == 0 else jnp.where(first, recv, keep)
        normed = (conv_out - mean_ref[half]) * scale_ref[half] + shift_ref[half]
        active = jnp.where(normed >= 0, normed, 0.01 * normed).astype(o_ref.dtype)
        o_ref[0, :, half * outs : (half + 1) * outs] = active


def normalize(ids, keep, recv, stats, gain, shift, cells):
    planes, rows, outs = keep.shape
    tile = 512
    spec = pltpu.PrefetchScalarGridSpec(
        num_scalar_prefetch=1,
        grid=(planes, rows // tile),
        in_specs=[pl.BlockSpec(memory_space=pltpu.VMEM)] * 5,
        out_specs=pl.BlockSpec((1, tile, 2 * outs), lambda i, j, ids: (i, j, 0)),
        scratch_shapes=[pltpu.VMEM((2, 1, outs), jnp.float32)] * 2,
    )
    return pl.pallas_call(
        functools.partial(norm_kernel, cells=cells),
        grid_spec=spec,
        out_shape=jax.ShapeDtypeStruct((planes, rows, 2 * outs), jnp.bfloat16),
        compiler_params=pltpu.CompilerParams(vmem_limit_bytes=32 << 20),
        cost_estimate=pl.CostEstimate(flops=4_000_000, bytes_accessed=3_000_000, transcendentals=0),
    )(ids, keep, recv, stats, gain, shift)


def chip_planes(slab, core):
    count = SIZES[2] * SIZES[3] * SIZES[4]
    pairs = []
    for d in range(count):
        to = d + 1 if d % 2 else d - 1
        if 0 <= to < count:
            pairs.append((d, to))
    edge = lax.dynamic_slice_in_dim(slab, core, 1, axis=0)
    halo = lax.ppermute(edge, DEPTH, pairs)
    mine = jnp.concatenate([halo, slab])
    other = lax.ppermute(mine, "c", SWAP)
    low = jnp.concatenate([mine, other[1:], other[:1]])
    high = jnp.concatenate([other, slab, halo])
    return jnp.where(core == 0, low, high)


def from_z(array, r):
    perm = []
    for here in range(8):
        there = (here + r) % 8
        for h in range(2):
            for xl in range(2):
                for c in range(2):
                    src = ((h * 8 + here) * 2 + xl) * 2 + c
                    if c == h:
                        dst = ((h * 8 + there) * 2 + xl) * 2 + c
                    else:
                        dst = (((1 - h) * 8 + there) * 2 + 1 - xl) * 2 + h
                    perm.append((src, dst))
    return lax.ppermute(array, ("xh", "z", "xl", "c"), perm)


def ring(array, axes, by):
    count = math.prod(SIZES[AXES.index(n)] for n in axes)
    return lax.ppermute(array, axes, [(i, (i + by) % count) for i in range(count)])


def put(buffer, piece, z, r, tap=0):
    where = jnp.remainder(z - r + 8, 8)
    return lax.dynamic_update_slice(buffer, piece[:, None], (tap, where, 0, 0))


def gather_weights(shard, core, widened):
    xh, zi, y, xl = (lax.axis_index(n) for n in ("xh", "z", "y", "xl"))
    to_xl = jnp.where(core == xh, xl, 1 - xl)
    part = lax.dynamic_slice_in_dim(shard, 13 * ((y + to_xl) % 2), 14, axis=0)
    xs, ys, zs = ("xh", "xl"), ("y",), ("z",)
    up, down, here = from_z(part, 1), from_z(part, -1), from_z(part, 0)
    up2, down2 = ring(up, zs, 1), ring(down, zs, -1)
    far_up, far_down = ring(jnp.stack([here, up, up2]), xs, 1), ring(jnp.stack([down, down2]), xs, -1)
    up3, down3 = ring(up2, zs, 1), ring(down2, zs, -1)
    top, bottom = ring(up3[:7], zs, 1), ring(down3[7:], zs, -1)
    wide = widened()
    top, bottom, wide = lax.optimization_barrier((top, bottom, wide))
    far_top = ring(jnp.concatenate([up3, top]), ys, 1)
    far_bottom = ring(jnp.concatenate([down3, bottom]), ys, -1)

    own = jnp.zeros((14, 8) + shard.shape[1:], shard.dtype)
    for r, piece in ((0, here), (1, up), (-1, down), (2, up2), (-2, down2), (3, up3), (-3, down3)):
        own = put(own, piece, zi, r)
    own = put(put(own, top, zi, 4), bottom, zi, 4, 7)
    merged = (14, 8 * shard.shape[1], shard.shape[2])

    def finish(gate):
        ups, downs, low, high, _ = lax.optimization_barrier((far_up, far_down, far_top, far_bottom, gate))
        other = jnp.zeros_like(own)
        for n in range(3):
            other = put(other, ups[n], zi, n)
        for n in range(2):
            other = put(other, downs[n], zi, -n - 1)
        other = put(put(other, low[:14], zi, 3), high[:14], zi, -3)
        other = put(put(other, low[14:], zi, 4), high[14:], zi, 4, 7)
        return other.reshape(merged)

    return own.reshape(merged), finish, wide


def local(slabs, kernel, gain, shift):
    core = lax.axis_index("c")
    z, y, xl = (lax.axis_index(n) for n in ("z", "y", "xl"))
    colour = (y + xl) % 2
    ids = jnp.stack([core, colour, z]).astype(jnp.int32)
    _, planes, height, width, chans = slabs.shape
    rows = height * width
    outs = chans // 2
    group = SIZES[2] * SIZES[3] * SIZES[4]

    shard = jnp.transpose(kernel, (0, 1, 2, 4, 3)).reshape(27, kernel.shape[4], chans)
    def widened():
        return widen(chip_planes(slabs[0].reshape(planes, rows, chans), core), width)

    own, finish, wide = gather_weights(shard, core, widened)
    acc = first_conv(ids, wide, own, rows, width)
    other = finish(acc)
    send, keep, stats = second_conv(ids, wide, other, acc, rows, width, group)
    recv = lax.ppermute(send, "c", SWAP)
    everyone = lax.all_to_all(stats, DEPTH, 0, 0, tiled=True)
    cells = planes * rows * group
    out = normalize(
        ids, keep, recv, everyone, gain.reshape(2, 1, outs), shift.reshape(2, 1, outs), cells
    )
    return out.reshape(slabs.shape)


def solution(mesh):
    fine = Mesh(mesh.devices.reshape(SIZES), AXES)
    x_spec = P(("xh", "z"), DEPTH, None, None, None)
    in_specs = (x_spec, P(None, None, None, None, ("xh", "z")), P(), P())
    return jax.shard_map(local, mesh=fine, in_specs=in_specs, out_specs=x_spec, check_vma=False)
```

```python
import functools
import math

import jax
import jax.numpy as jnp
from jax import lax
from jax.experimental import pallas as pl
from jax.experimental.pallas import tpu as pltpu
from jax.sharding import Mesh, PartitionSpec as P

AXES = ("xh", "z", "y", "xl", "c")
SIZES = (2, 8, 4, 2, 2)
CHIPS = ("y", "xl")
DEPTH = ("y", "xl", "c")
SWAP = [(0, 1), (1, 0)]
EPS = 1e-05
PADDED = 256

def shift_rows(plane, by, width):
    rows = plane.shape[0]
    moved = pltpu.roll(plane, by % rows, 0)
    w = lax.broadcasted_iota(jnp.int32, plane.shape, 0) % width
    edge = 0 if by == 1 else width - 1
    return jnp.where(w == edge, 0.0, moved)


def widen_kernel(x_ref, o_ref, *, width):
    for n in range(x_ref.shape[0]):
        x = x_ref[n]
        rows, chans = x.shape
        zero = jnp.zeros((width, 3 * chans), o_ref.dtype)
        o_ref[n, 0:width, :] = zero
        o_ref[n, width + rows : 2 * width + rows, :] = zero
        wide = x.astype(jnp.float32)
        o_ref[n, width : width + rows, 0:chans] = shift_rows(wide, 1, width).astype(o_ref.dtype)
        o_ref[n, width : width + rows, chans : 2 * chans] = x
        o_ref[n, width : width + rows, 2 * chans : 3 * chans] = shift_rows(wide, -1, width).astype(o_ref.dtype)


def widen(planes, width):
    count, rows, chans = planes.shape
    return pl.pallas_call(
        functools.partial(widen_kernel, width=width),
        grid=(count // 3,),
        in_specs=[pl.BlockSpec((3, rows, chans), lambda i: (i, 0, 0))],
        out_specs=pl.BlockSpec((3, rows + 2 * width, 3 * chans), lambda i: (i, 0, 0)),
        out_shape=jax.ShapeDtypeStruct((count, rows + 2 * width, 3 * chans), planes.dtype),
        compiler_params=pltpu.CompilerParams(vmem_limit_bytes=32 << 20),
        cost_estimate=pl.CostEstimate(flops=0, bytes_accessed=12_000_000, transcendentals=0),
    )(planes)


def half_conv(x_ref, w_ref, plane, taps, rows, width):
    chans = w_ref.shape[2]
    lhs, rhs = [], []
    for i, t in taps:
        a, b, e = t // 9, t // 3 % 3, t % 3
        lhs.append(x_ref[plane + a, b * width : b * width + rows, e * chans : (e + 1) * chans])
        rhs.append(w_ref[i])
    lhs, rhs = jnp.concatenate(lhs, axis=1), jnp.concatenate(rhs, axis=1)
    return lax.dot_general(lhs, rhs, (((1,), (1,)), ((), ())), preferred_element_type=jnp.float32)


LOW_TAPS = [(t, t) for t in range(14)]
HIGH_TAPS = [(t - 13, t) for t in range(14, 27)]


def first_kernel(ids_ref, x_ref, w_ref, acc_ref, *, rows, width):
    core, colour = ids_ref[0], ids_ref[1]

    def run(taps):
        for j in range(4):
            plane = (j + 2 * (1 - core)) % 4
            acc_ref[j] = half_conv(x_ref, w_ref, plane, taps, rows, width)

    pl.when(colour == 0)(lambda: run(LOW_TAPS))
    pl.when(colour != 0)(lambda: run(HIGH_TAPS))


def second_kernel(ids_ref, x_ref, w_ref, acc_ref, send_ref, keep_ref, stats_ref, sum_ref, *, rows, width):
    core, colour = ids_ref[0], ids_ref[1]
    outs = acc_ref.shape[2]
    sum_ref[...] = jnp.zeros_like(sum_ref)

    def run(taps):
        for j in range(4):
            plane = (j + 2 * (1 - core)) % 4
            total = acc_ref[j] + half_conv(x_ref, w_ref, plane, taps, rows, width)
            sum_ref[0:1, :] += jnp.sum(total, axis=0, keepdims=True)
            sum_ref[1:2, :] += jnp.sum(total * total, axis=0, keepdims=True)
            if j < 2:
                send_ref[j, :, 0:outs] = total
                send_ref[j, :, outs:] = jnp.zeros((rows, send_ref.shape[2] - outs), jnp.float32)
            else:
                keep_ref[j - 2] = total

    pl.when(colour == 0)(lambda: run(HIGH_TAPS))
    pl.when(colour != 0)(lambda: run(LOW_TAPS))
    row = jnp.concatenate([sum_ref[0:1, :], sum_ref[1:2, :]], axis=1)
    stats_ref[...] = jnp.broadcast_to(row[None], stats_ref.shape)


def in_vmem(kernel, count, out_shape, scratch, flops, limit):
    whole = pl.BlockSpec(memory_space=pltpu.VMEM)
    outs = [whole] * len(out_shape)
    return pl.pallas_call(
        kernel,
        grid_spec=pltpu.PrefetchScalarGridSpec(
            num_scalar_prefetch=1, grid=(), in_specs=[whole] * count, out_specs=outs, scratch_shapes=scratch
        ),
        out_shape=out_shape,
        compiler_params=pltpu.CompilerParams(vmem_limit_bytes=limit << 20),
        cost_estimate=pl.CostEstimate(flops=flops, bytes_accessed=8_000_000, transcendentals=0),
    )


def first_conv(ids, wide, own, rows, width):
    kernel = functools.partial(first_kernel, rows=rows, width=width)
    out = [jax.ShapeDtypeStruct((4, rows, own.shape[1]), jnp.float32)]
    return in_vmem(kernel, 2, out, [], 5 * 10**9, 40)(ids, wide, own)[0]


def second_conv(ids, wide, other, acc, rows, width, group):
    outs = other.shape[1]
    kernel = functools.partial(second_kernel, rows=rows, width=width)
    shapes = ((2, rows, PADDED), (2, rows, outs), (group, 1, 2 * outs))
    out = [jax.ShapeDtypeStruct(shape, jnp.float32) for shape in shapes]
    scratch = [pltpu.VMEM((8, outs), jnp.float32)]
    return in_vmem(kernel, 3, out, scratch, 5 * 10**9, 40)(ids, wide, other, acc)


def norm_kernel(ids_ref, keep_ref, recv_ref, stats_ref, gain_ref, shift_ref, o_ref, mean_ref, scale_ref, *, cells):
    first = ids_ref[0] == 0
    outs = keep_ref.shape[2]
    plane, tile = pl.program_id(0), o_ref.shape[1]

    @pl.when((plane == 0) & (pl.program_id(1) == 0))
    def _():
        for half in range(2):
            sums = stats_ref[half]
            for chip in range(1, stats_ref.shape[0] // 2):
                sums = sums + stats_ref[2 * chip + half]
            mean = sums[:, 0:outs] / cells
            variance = sums[:, outs : 2 * outs] / cells - mean * mean
            mean_ref[half] = mean
            scale_ref[half] = gain_ref[half] / jnp.sqrt(variance + EPS)

    where = pl.ds(pl.multiple_of(pl.program_id(1) * tile, tile), tile)
    keep, recv = keep_ref[plane, where, :], recv_ref[plane, where, 0:outs]
    for half in range(2):
        conv_out = jnp.where(first, keep, recv) if half == 0 else jnp.where(first, recv, keep)
        normed = (conv_out - mean_ref[half]) * scale_ref[half] + shift_ref[half]
        active = jnp.where(normed >= 0, normed, 0.01 * normed).astype(o_ref.dtype)
        o_ref[0, :, half * outs : (half + 1) * outs] = active


def normalize(ids, keep, recv, stats, gain, shift, cells):
    planes, rows, outs = keep.shape
    tile = 512
    spec = pltpu.PrefetchScalarGridSpec(
        num_scalar_prefetch=1,
        grid=(planes, rows // tile),
        in_specs=[pl.BlockSpec(memory_space=pltpu.VMEM)] * 5,
        out_specs=pl.BlockSpec((1, tile, 2 * outs), lambda i, j, ids: (i, j, 0)),
        scratch_shapes=[pltpu.VMEM((2, 1, outs), jnp.float32)] * 2,
    )
    return pl.pallas_call(
        functools.partial(norm_kernel, cells=cells),
        grid_spec=spec,
        out_shape=jax.ShapeDtypeStruct((planes, rows, 2 * outs), jnp.bfloat16),
        compiler_params=pltpu.CompilerParams(vmem_limit_bytes=32 << 20),
        cost_estimate=pl.CostEstimate(flops=4_000_000, bytes_accessed=3_000_000, transcendentals=0),
    )(ids, keep, recv, stats, gain, shift)


def chip_planes(slab, core):
    count = SIZES[2] * SIZES[3] * SIZES[4]
    pairs = []
    for d in range(count):
        to = d + 1 if d % 2 else d - 1
        if 0 <= to < count:
            pairs.append((d, to))
    edge = lax.dynamic_slice_in_dim(slab, core, 1, axis=0)
    halo = lax.ppermute(edge, DEPTH, pairs)
    mine = jnp.concatenate([halo, slab])
    other = lax.ppermute(mine, "c", SWAP)
    low = jnp.concatenate([mine, other[1:], other[:1]])
    high = jnp.concatenate([other, slab, halo])
    return jnp.where(core == 0, low, high)


def from_z(array, r):
    perm = []
    for here in range(8):
        there = (here + r) % 8
        for h in range(2):
            for xl in range(2):
                for c in range(2):
                    src = ((h * 8 + here) * 2 + xl) * 2 + c
                    if c == h:
                        dst = ((h * 8 + there) * 2 + xl) * 2 + c
                    else:
                        dst = (((1 - h) * 8 + there) * 2 + 1 - xl) * 2 + h
                    perm.append((src, dst))
    return lax.ppermute(array, ("xh", "z", "xl", "c"), perm)


def ring(array, axes, by):
    count = math.prod(SIZES[AXES.index(n)] for n in axes)
    return lax.ppermute(array, axes, [(i, (i + by) % count) for i in range(count)])


def put(buffer, piece, z, r, tap=0):
    where = jnp.remainder(z - r + 8, 8)
    return lax.dynamic_update_slice(buffer, piece[:, None], (tap, where, 0, 0))


def gather_weights(shard, core, widened):
    xh, zi, y, xl = (lax.axis_index(n) for n in ("xh", "z", "y", "xl"))
    to_xl = jnp.where(core == xh, xl, 1 - xl)
    part = lax.dynamic_slice_in_dim(shard, 13 * ((y + to_xl) % 2), 14, axis=0)
    xs, ys, zs = ("xh", "xl"), ("y",), ("z",)
    up, down, here = from_z(part, 1), from_z(part, -1), from_z(part, 0)
    up2, down2 = ring(up, zs, 1), ring(down, zs, -1)
    far_up, far_down = ring(jnp.stack([here, up, up2]), xs, 1), ring(jnp.stack([down, down2]), xs, -1)
    up3, down3 = ring(up2, zs, 1), ring(down2, zs, -1)
    top, bottom = ring(up3[:7], zs, 1), ring(down3[7:], zs, -1)
    wide = widened()
    top, bottom, wide = lax.optimization_barrier((top, bottom, wide))
    far_top = ring(jnp.concatenate([up3, top]), ys, 1)
    far_bottom = ring(jnp.concatenate([down3, bottom]), ys, -1)

    own = jnp.zeros((14, 8) + shard.shape[1:], shard.dtype)
    for r, piece in ((0, here), (1, up), (-1, down), (2, up2), (-2, down2), (3, up3), (-3, down3)):
        own = put(own, piece, zi, r)
    own = put(put(own, top, zi, 4), bottom, zi, 4, 7)
    merged = (14, 8 * shard.shape[1], shard.shape[2])

    def finish(gate):
        ups, downs, low, high, _ = lax.optimization_barrier((far_up, far_down, far_top, far_bottom, gate))
        other = jnp.zeros_like(own)
        for n in range(3):
            other = put(other, ups[n], zi, n)
        for n in range(2):
            other = put(other, downs[n], zi, -n - 1)
        other = put(put(other, low[:14], zi, 3), high[:14], zi, -3)
        other = put(put(other, low[14:], zi, 4), high[14:], zi, 4, 7)
        return other.reshape(merged)

    return own.reshape(merged), finish, wide


def local(slabs, kernel, gain, shift):
    core = lax.axis_index("c")
    z, y, xl = (lax.axis_index(n) for n in ("z", "y", "xl"))
    colour = (y + xl) % 2
    ids = jnp.stack([core, colour, z]).astype(jnp.int32)
    _, planes, height, width, chans = slabs.shape
    rows = height * width
    outs = chans // 2
    group = SIZES[2] * SIZES[3] * SIZES[4]

    shard = jnp.transpose(kernel, (0, 1, 2, 4, 3)).reshape(27, kernel.shape[4], chans)
    def widened():
        return widen(chip_planes(slabs[0].reshape(planes, rows, chans), core), width)

    own, finish, wide = gather_weights(shard, core, widened)
    acc = first_conv(ids, wide, own, rows, width)
    other = finish(acc)
    send, keep, stats = second_conv(ids, wide, other, acc, rows, width, group)
    recv = lax.ppermute(send, "c", SWAP)
    everyone = lax.all_to_all(stats, DEPTH, 0, 0, tiled=True)
    cells = planes * rows * group
    out = normalize(
        ids, keep, recv, everyone, gain.reshape(2, 1, outs), shift.reshape(2, 1, outs), cells
    )
    return out.reshape(slabs.shape)


def solution(mesh):
    fine = Mesh(mesh.devices.reshape(SIZES), AXES)
    x_spec = P(("xh", "z"), DEPTH, None, None, None)
    in_specs = (x_spec, P(None, None, None, None, ("xh", "z")), P(), P())
    return jax.shard_map(local, mesh=fine, in_specs=in_specs, out_specs=x_spec, check_vma=False)
```
